256 devices in a mesh: dp: 4 (over y), expert: 64 (over x, z, core).
Axes of the slice: x: 4, y: 4, z: 8, core: 2. Of those that a mesh axis runs over, the one named last changes fastest.
Arguments:
- tokens: bfloat16 [8192, 2048], P(('dp', 'expert')), may hold values from -6 to 6
- grad_out: bfloat16 [8192, 2048], P(('dp', 'expert')), may hold values from -0.59765625 to 0.59765625
- routing: int32 [8192, 8], P(('dp', 'expert')), may hold values from 0 to 127, as said below
- replica: int32 [8192, 8], P(('dp', 'expert')), may hold values from 0 to 1, as said below
- gates: bfloat16 [8192, 8], P(('dp', 'expert')), may hold values from 0.25 to 4
- host_expert: int32 [64], replicated, may hold values from 0 to 127, as said below
- w_gate_up: bfloat16 [128, 2, 768, 2048], P('expert', None, 'dp'), may hold values from -0.125 to 0.125
- w_down: bfloat16 [128, 768, 2048], P('expert', 'dp'), may hold values from -0.21875 to 0.21875
Outputs:
- grad_tokens: bfloat16 [8192, 2048], P(('dp', 'expert'))
- grad_gates: float32 [8192, 8], P(('dp', 'expert'))
- grad_w_gate_up: bfloat16 [128, 2, 768, 2048], P('expert', None, 'dp')
- grad_w_down: bfloat16 [128, 768, 2048], P('expert', 'dp')
The draws below stay inside these ranges and needn't reach their ends.
Inputs may be any that keep to these rules, and one draw needn't show every extreme that they name: `routing`: column k of a token names an expert of 16 * k to 16 * k + 15. Within the rows of one device, experts 2 i and 2 i + 1 are named together exactly 2 * 2 times. `replica`: within the rows of one device, each expert has at most 2 choices marked 0 and at most 2 marked 1; some expert reaches 2 marked 0 from every device, and in every index of dp some expert reaches 2 marked 1 from every device. Only experts listed in host_expert have choices marked 1. `host_expert`: for every device d of the expert axis exactly one of its experts 2 d and 2 d + 1 is listed, and it is listed once.
All inputs are finite; a program needn't handle non-finite values.
Results may differ from the reference program's by a relative error of at most 0.013.
Values may be sent and summed in bfloat16 or wider, within the bound.
No kernel may reach another device: no remote copies, remote signals or barrier semaphores. Data moves between devices by JAX's collectives and lax.ppermute only.
A program may use at most 128 MiB of HBM per device.

```python
import jax
import jax.numpy as jnp
from jax import lax

D = 2048
FF = 768
TOPK = 8
TOK_DEV = 32
EXPERTS = 128
TOKENS = 8192
BAND = 16
SLOT = 2
BLOCK = 128
N_DP = 4
N_EXPERT = 64


def routing_layout(key):
    root_key = jax.random.fold_in(key, 4242)
    subkeys = jax.random.split(root_key, 5)
    pairs_all = N_EXPERT
    plus_bit = jax.random.randint(subkeys[0], (pairs_all,), 0, 2).astype(jnp.int32)
    extra_share = jax.random.randint(subkeys[1], (N_DP, N_EXPERT, pairs_all), 0, SLOT + 1).astype(jnp.int32)
    full_pair = jax.random.randint(subkeys[2], (N_DP, 1, 1), 0, pairs_all).astype(jnp.int32)
    pair_iota = lax.broadcasted_iota(jnp.int32, (N_DP, N_EXPERT, pairs_all), 2)
    extra_share = jnp.where(pair_iota == full_pair, SLOT, extra_share)
    layout_shape = (N_DP, N_EXPERT, TOPK, TOK_DEV)
    position = lax.broadcasted_iota(jnp.int32, layout_shape, 3)
    column = lax.broadcasted_iota(jnp.int32, layout_shape, 2)
    pair_ids = column * (BAND // 2) + position // (2 * SLOT)
    within = position % (2 * SLOT)
    extra_rows = jnp.take_along_axis(extra_share, pair_ids.reshape(N_DP, N_EXPERT, TOPK * TOK_DEV), axis=2).reshape(layout_shape)
    plus_side = within < SLOT + extra_rows
    chosen_bit = jnp.take(plus_bit, pair_ids)
    expert = 2 * pair_ids + jnp.where(plus_side, chosen_bit, 1 - chosen_bit)
    copy_flag = ((within >= SLOT) & plus_side).astype(jnp.int32)
    scores = jax.random.randint(subkeys[3], layout_shape, 0, 1048576).astype(jnp.int32) * TOK_DEV + position
    ordering = jnp.argsort(scores, axis=3, stable=True).astype(jnp.int32)
    expert = jnp.take_along_axis(expert, ordering, axis=3)
    copy_flag = jnp.take_along_axis(copy_flag, ordering, axis=3)
    routing = jnp.transpose(expert, (0, 1, 3, 2)).reshape(N_DP * N_EXPERT * TOK_DEV, TOPK).astype(jnp.int32)
    replica = jnp.transpose(copy_flag, (0, 1, 3, 2)).reshape(N_DP * N_EXPERT * TOK_DEV, TOPK).astype(jnp.int32)
    owners = jax.random.permutation(subkeys[4], N_EXPERT).astype(jnp.int32)
    host_list = (2 * owners + jnp.take(plus_bit, owners)).astype(jnp.int32)
    return (routing, replica, host_list)


def draw_routing(key, part):
    return routing_layout(key)[0]


def draw_replica(key, part):
    return routing_layout(key)[1]


def draw_host_expert(key, part):
    return routing_layout(key)[2]


def level_of(key, shape, cuts, low, top_value):
    loudness = 1.0
    for axis_at, shards_of in cuts:
        heights = jax.random.uniform(jax.random.fold_in(jax.random.fold_in(key, 6), axis_at), (shards_of,), jnp.float32, low / len(cuts), top_value / len(cuts))
        loudness = loudness * jnp.repeat(jnp.exp(heights), shape[axis_at] // shards_of).reshape((-1,) + (1,) * (len(shape) - 1 - axis_at))
    return loudness


def gaussian(stream_key, shape, deviation, most, pieces=(), kind=jnp.bfloat16):
    drawn = jax.random.normal(stream_key, shape, jnp.float32) * deviation
    if len(pieces) > 0:
        drawn = level_of(stream_key, shape, pieces, -0.22, 0.18) * drawn
    return jnp.clip(drawn, min=-most, max=most).astype(kind)


def setup_inputs(seed: int = 0) -> dict:
    key_list = jax.random.split(jax.random.key(seed), 9)
    return {
        "tokens": gaussian(key_list[0], (TOKENS, D), 1.0, 6.0, ((0, 256),)),
        "grad_out": gaussian(key_list[1], (TOKENS, D), 0.1, 0.59765625, ((0, 256),)),
        "routing": draw_routing(jax.random.fold_in(key_list[8], 71), 0),
        "replica": draw_replica(jax.random.fold_in(key_list[8], 71), 0),
        "gates": jnp.clip(0.25 + 3.75 * jax.random.uniform(key_list[4], (TOKENS, TOPK), jnp.float32) ** level_of(key_list[4], (TOKENS, TOPK), ((0, 256),), -0.2, 0.2), 0.25, 4.0).astype(jnp.bfloat16),
        "host_expert": draw_host_expert(jax.random.fold_in(key_list[8], 71), 0),
        "w_gate_up": gaussian(key_list[6], (EXPERTS, 2, FF, D), D ** -0.5, 0.125, ((0, 64), (2, 4))),
        "w_down": gaussian(key_list[7], (EXPERTS, FF, D), FF ** -0.5, 0.21875, ((0, 64), (1, 4))),
    }


def expert_pass(tokens, grad_out, gates, row_ids, live_rows, gate_up_w, down_w):
    token_ids = row_ids // TOPK
    live_mask = live_rows.astype(tokens.dtype)
    inputs = tokens[token_ids] * live_mask[:, None]
    upstream = grad_out[token_ids] * live_mask[:, None]
    weight = gates.reshape(-1)[row_ids] * live_mask
    quarter = FF // N_DP
    gate_up = gate_up_w.astype(jnp.float32).reshape(2, N_DP, quarter, D)
    down_matrix = down_w.astype(jnp.float32).reshape(N_DP, quarter, D)
    highest = lax.Precision.HIGHEST
    mixed_pre = jnp.einsum("rd,jqfd->rjqf", inputs.astype(jnp.float32), gate_up, precision=highest)
    gate_pre = mixed_pre[:, 0]
    up_part = mixed_pre[:, 1]
    sigmoid_gate = jax.nn.sigmoid(gate_pre)
    active = gate_pre * sigmoid_gate
    hidden = (active * up_part).astype(jnp.bfloat16)
    output_part = jnp.einsum("rqf,qfd->qrd", hidden.astype(jnp.float32), down_matrix, precision=highest)
    gate_part = jnp.sum(output_part * upstream.astype(jnp.float32)[None], axis=2).astype(jnp.bfloat16)
    row_dg = jnp.sum(gate_part.astype(jnp.float32), axis=0).astype(jnp.bfloat16)
    scaled = (weight.astype(jnp.float32)[:, None] * upstream.astype(jnp.float32)).astype(jnp.bfloat16)
    grad_hidden = jnp.einsum("rd,qfd->rqf", scaled.astype(jnp.float32), down_matrix, precision=highest)
    grad_gate = grad_hidden * up_part * sigmoid_gate * (1.0 + gate_pre * (1.0 - sigmoid_gate))
    grad_mixed = jnp.stack([grad_gate, grad_hidden * active], axis=1).astype(jnp.bfloat16)
    input_part = jnp.einsum("rjqf,jqfd->qrd", grad_mixed.astype(jnp.float32), gate_up, precision=highest)
    row_dx = jnp.sum(input_part.astype(jnp.bfloat16).astype(jnp.float32), axis=0).astype(jnp.bfloat16)
    weight_gu = jnp.einsum("rd,rjqf->jqfd", inputs.astype(jnp.float32), grad_mixed.astype(jnp.float32), precision=highest)
    weight_down = jnp.einsum("rqf,rd->qfd", hidden.astype(jnp.float32), scaled.astype(jnp.float32), precision=highest)
    return row_dx, row_dg, weight_gu.reshape(2, FF, D), weight_down.reshape(FF, D)


def reference(tokens, grad_out, routing, replica, gates, host_expert, w_gate_up, w_down):
    expert_ids = lax.broadcasted_iota(jnp.int32, (EXPERTS, N_EXPERT), 0)
    helper_ids = lax.broadcasted_iota(jnp.int32, (EXPERTS, N_EXPERT), 1)
    matches = host_expert[None, :] == expert_ids
    listed = jnp.sum(matches.astype(jnp.int32), axis=1)
    helper_of = jnp.sum(jnp.where(matches, helper_ids, 0), axis=1).astype(jnp.int32)
    flat_route = routing.reshape(-1).astype(jnp.int32)
    flat_copy = replica.reshape(-1).astype(jnp.int32)
    usable = (flat_copy == 0) | (listed[flat_route] > 0)
    labels = jnp.where(usable, flat_copy * EXPERTS + flat_route, 2 * EXPERTS).astype(jnp.int32)
    ordering = jnp.argsort(labels, stable=True).astype(jnp.int32)
    counts = jnp.bincount(labels, length=2 * EXPERTS + 1).astype(jnp.int32)
    starts = (jnp.cumsum(counts) - counts).astype(jnp.int32)
    capacity = N_DP * BLOCK
    padded = jnp.concatenate([ordering, jnp.zeros((capacity,), jnp.int32)])

    def segment(label_id):
        row_ids = lax.dynamic_slice_in_dim(padded, starts[label_id], capacity).astype(jnp.int32)
        live_rows = lax.broadcasted_iota(jnp.int32, (capacity,), 0) < counts[label_id]
        return row_ids, live_rows

    def accumulate(totals, row_ids, live_rows, row_dx, row_dg):
        grad_tok, grad_row = totals
        live_mask = live_rows.astype(jnp.float32)
        grad_tok = grad_tok.at[row_ids // TOPK].add(row_dx.astype(jnp.float32) * live_mask[:, None])
        grad_row = grad_row.at[row_ids].add(row_dg.astype(jnp.float32) * live_mask)
        return grad_tok, grad_row

    def helper_step(totals, expert):
        row_ids, live_rows = segment(EXPERTS + expert)
        row_dx, row_dg, weight_gu, weight_down = expert_pass(tokens, grad_out, gates, row_ids, live_rows, w_gate_up[expert], w_down[expert])
        totals = accumulate(totals, row_ids, live_rows, row_dx, row_dg)
        return totals, (weight_gu.astype(jnp.bfloat16), weight_down.astype(jnp.bfloat16))

    start_totals = (jnp.zeros((TOKENS, D), jnp.float32), jnp.zeros((TOKENS * TOPK,), jnp.float32))
    totals, helper_parts = lax.scan(helper_step, start_totals, host_expert.astype(jnp.int32))
    helper_gu, helper_down = helper_parts

    def owner_step(totals, expert):
        row_ids, live_rows = segment(expert)
        row_dx, row_dg, weight_gu, weight_down = expert_pass(tokens, grad_out, gates, row_ids, live_rows, w_gate_up[expert], w_down[expert])
        totals = accumulate(totals, row_ids, live_rows, row_dx, row_dg)
        present = (listed[expert] > 0).astype(jnp.float32)
        extra_gu = helper_gu[helper_of[expert]].astype(jnp.float32) * present
        extra_down = helper_down[helper_of[expert]].astype(jnp.float32) * present
        return totals, ((weight_gu + extra_gu).astype(jnp.bfloat16), (weight_down + extra_down).astype(jnp.bfloat16))

    totals, owner_parts = lax.scan(owner_step, totals, jnp.arange(EXPERTS, dtype=jnp.int32))
    grad_tok, grad_row = totals
    grad_w_gate_up, grad_w_down = owner_parts
    return grad_tok.astype(jnp.bfloat16), grad_row.reshape(TOKENS, TOPK), grad_w_gate_up, grad_w_down
```

```python
import functools

import jax
import jax.numpy as jnp
from jax import lax
from jax.experimental import pallas as pl
from jax.experimental.pallas import tpu as pltpu
from jax.sharding import PartitionSpec as P

LANES = 128
MIB = 1 << 20
NT = (((1,), (1,)), ((), ()))
TN = (((0,), (0,)), ((), ()))
NN = (((1,), (0,)), ((), ()))


def dot(a, b, dims):
    return lax.dot_general(a, b, dims, preferred_element_type=jnp.float32)


def iota(shape, dim):
    return lax.broadcasted_iota(jnp.int32, shape, dim)


def to_column(row):
    n = row.shape[1]
    eye = iota((n, n), 0) == iota((n, n), 1)
    return jnp.sum(jnp.where(eye, jnp.broadcast_to(row, (n, n)), 0), axis=1, keepdims=True)


def dispatch_kernel(
    chunks, devices, routing, replica, gates, host, tokens, grad_out, *outs
):
    *row_refs, picker_ref, slots_ref = outs
    topk, count = routing.shape
    features = tokens.shape[1]
    total = topk * count
    per_pair = total // devices
    part = per_pair // chunks
    host_col = to_column(host[...])
    lanes_of = iota((count, total), 1)
    rows_of = iota((total, count), 0)
    earlier = iota((count, count), 0)
    gate_at = jnp.zeros((total, count), jnp.float32)
    first_at = jnp.zeros((total, count), jnp.float32)
    picked = jnp.zeros((total, count), jnp.float32)
    picked_t = jnp.zeros((count, total), jnp.float32)
    for k in range(topk):
        expert = routing[k : k + 1, :]
        dest = lax.shift_right_logical(expert, 1)
        listed = jnp.max((host_col == expert).astype(jnp.int32), axis=0, keepdims=True)
        usable = (replica[k : k + 1, :] == 0) | (listed > 0)
        key = (1 - listed) * count + iota((1, count), 1)
        dest_col, key_col = to_column(dest), to_column(key)
        ahead = (dest_col == dest) & (key_col < key)
        rank = jnp.sum(ahead.astype(jnp.int32), axis=0, keepdims=True)
        slot = (rank // part) * (devices * part) + dest * part + rank % part
        slot = jnp.where(usable, slot, -1)
        slots_ref[k : k + 1, :] = slot
        match = rows_of == slot
        picked = jnp.where(match, 1.0, picked)
        gate_at = jnp.where(match, gates[k : k + 1, :], gate_at)
        first_at = jnp.where(match, listed.astype(jnp.float32), first_at)
        picked_t = jnp.where(lanes_of == to_column(slot), 1.0, picked_t)
    picker_ref[...] = picked_t.astype(jnp.bfloat16)
    any_row = jnp.sum(picked, axis=1, keepdims=True)
    gate = jnp.sum(gate_at, axis=1, keepdims=True)
    first = jnp.sum(first_at, axis=1, keepdims=True)
    second = any_row - first
    lane = iota((total, LANES), 1)
    meta = jnp.where(lane == 0, gate * first, 0.0)
    meta = jnp.where(lane == 1, gate * second, meta)
    meta = jnp.where(lane == 2, first, meta)
    meta = jnp.where(lane == 3, second, meta).astype(jnp.bfloat16)
    picker = picked.astype(jnp.bfloat16)
    size = total // chunks
    for c, out in enumerate(row_refs):
        mine = slice(c * size, (c + 1) * size)
        out[:, :features] = dot(picker[mine], tokens[...], NN).astype(jnp.bfloat16)
        out[:, features : 2 * features] = dot(picker[mine], grad_out[...], NN).astype(jnp.bfloat16)
        out[:, 2 * features :] = meta[mine]


def pieces_of(refs, start, size, cols):
    got, at = [], 0
    for r in refs:
        low, high = max(start, at), min(start + size, at + r.shape[0])
        if low < high:
            got.append(r[low - at : high - at, cols])
        at += r.shape[0]
    return got[0] if len(got) == 1 else jnp.concatenate(got, axis=0)


def put_pieces(refs, start, cols, value):
    at = 0
    for r in refs:
        low, high = max(start, at), min(start + value.shape[0], at + r.shape[0])
        if low < high:
            r[low - at : high - at, cols] = value[low - start : high - start]
        at += r.shape[0]


def expert_kernel(experts, n_in, n_out, order, *refs):
    pieces = refs[:n_in]
    gu = refs[n_in : n_in + experts]
    down = refs[n_in + experts : n_in + 2 * experts]
    outs = refs[n_in + 2 * experts : n_in + 2 * experts + n_out]
    gm_ref, hg_ref = refs[n_in + 2 * experts + n_out :]
    quarter, features = down[0].shape[1:]
    width = experts * quarter
    rows = sum(p.shape[0] for p in pieces)
    block = min(rows, 256)

    def stack(parts):
        return parts[0] if experts == 1 else jnp.concatenate(parts, axis=0)

    w_gate = stack([w[0, 0] for w in gu])
    w_up = stack([w[0, 1] for w in gu])
    w_down = stack([w[0] for w in down])
    for at in range(0, rows, block):
        x = pieces_of(pieces, at, block, slice(0, features))
        dy = pieces_of(pieces, at, block, slice(features, 2 * features))
        meta = pieces_of(pieces, at, block, slice(2 * features, 2 * features + LANES)).astype(jnp.float32)
        weight, live = meta[:, 0:1], meta[:, 2:3]
        if experts == 2:
            is_first = iota((block, width), 1) < quarter
            weight = jnp.where(is_first, weight, meta[:, 1:2])
            live = jnp.where(is_first, live, meta[:, 3:4])
        gate = dot(x, w_gate, NT)
        up = dot(x, w_up, NT)
        back = dot(dy, w_down, NT)
        s = jax.nn.sigmoid(gate)
        active = gate * s
        hidden = (active * up).astype(jnp.bfloat16).astype(jnp.float32)
        dg = jnp.sum(hidden * back * live, axis=1, keepdims=True)
        grad_hidden = back * weight
        gm_gate = (grad_hidden * up * s * (1.0 + gate * (1.0 - s))).astype(jnp.bfloat16)
        gm_up = (grad_hidden * active).astype(jnp.bfloat16)
        gm_ref[at : at + block, :width] = gm_gate
        gm_ref[at : at + block, width:] = gm_up
        hg_ref[at : at + block] = (hidden * weight).astype(jnp.bfloat16)
        dx = dot(gm_gate, w_gate, NN) + dot(gm_up, w_up, NN)
        put_pieces(outs, at, slice(0, features), dx.astype(jnp.bfloat16))
        put_pieces(
            outs,
            at,
            slice(features, features + LANES),
            jnp.broadcast_to(dg, (block, LANES)).astype(jnp.bfloat16),
        )


def weights_kernel(n, order, *refs):
    x0, x1, dy0, dy1 = (refs[i * n : (i + 1) * n] for i in range(4))
    gm0, hg0, gm1, hg1, out_gu, out_down = refs[4 * n :]
    q = hg0.shape[1]
    first = order[0]
    second = 1 - first

    def whole(parts):
        return jnp.concatenate([p[...] for p in parts], axis=0)

    a = dot(gm0[...], whole(x0), TN)
    b = dot(gm1[...], whole(x1), TN)
    for j in range(2):
        out_gu[first, j] = (a[j * q : (j + 1) * q] + b[2 * j * q : (2 * j + 1) * q]).astype(jnp.bfloat16)
        out_gu[second, j] = b[(2 * j + 1) * q : (2 * j + 2) * q].astype(jnp.bfloat16)
    a = dot(hg0[...], whole(dy0), TN)
    b = dot(hg1[...], whole(dy1), TN)
    out_down[first] = (a + b[:q]).astype(jnp.bfloat16)
    out_down[second] = b[q:].astype(jnp.bfloat16)


def home_kernel(chunks, picker, slots, *refs):
    rows, (tok_ref, gate_ref) = refs[:chunks], refs[chunks:]
    features = tok_ref.shape[1]
    topk, count = slots.shape
    size = rows[0].shape[0]
    total = jnp.zeros((count, features), jnp.float32)
    for c, r in enumerate(rows):
        total += dot(picker[:, c * size : (c + 1) * size], r[:, :features], NN)
    tok_ref[...] = total.astype(jnp.bfloat16)
    dg = jnp.concatenate([r[:, features : features + LANES] for r in rows], axis=0).astype(jnp.float32)[:, :1]
    rows_of = iota((chunks * size, count), 0)
    for k in range(topk):
        match = rows_of == slots[k : k + 1, :]
        gate_ref[k : k + 1, :] = jnp.sum(jnp.where(match, dg, 0.0), axis=0, keepdims=True)


def shift(x, step):
    n = lax.axis_size("dp")
    return lax.ppermute(x, "dp", [(i, (i + step) % n) for i in range(n)])


def spread(x):
    half = x.shape[0] // 2
    left, right = shift(x, 1), shift(x, -1)
    return (x, left, right, shift(left[:half], 1), shift(right[half:], -1))


def add(a, b):
    return (a.astype(jnp.float32) + b.astype(jnp.float32)).astype(jnp.bfloat16)


def collect(own, left1, left2, right1, right2, far1, far2):
    from_left1 = shift(add(right1, shift(far1, 1)), 1)
    from_left2 = shift(right2, 1)
    from_right1 = shift(left1, -1)
    from_right2 = shift(add(left2, shift(far2, -1)), -1)
    total = own.astype(jnp.float32)
    total += jnp.concatenate([from_left1, from_left2], axis=0).astype(jnp.float32)
    total += jnp.concatenate([from_right1, from_right2], axis=0).astype(jnp.float32)
    return total.astype(jnp.bfloat16)


def exchange(x):
    return lax.all_to_all(x, "expert", split_axis=0, concat_axis=0, tiled=True)


def shards(tokens, grad_out, routing, replica, gates, host_expert, w_gate_up, w_down):
    devices = lax.axis_size("expert")
    device_id = lax.axis_index("expert")
    count, features = tokens.shape
    topk = routing.shape[1]
    owned, quarter = w_down.shape[:2]
    chunks = 2
    total = count * topk
    size = total // chunks
    wide = 2 * features + LANES
    bf16 = jnp.bfloat16

    first = jnp.sum(jnp.where(host_expert // owned == device_id, host_expert % owned, 0))
    order = first.astype(jnp.int32).reshape(1)

    *sent, picker, slots = pl.pallas_call(
        functools.partial(dispatch_kernel, chunks, devices),
        out_shape=[jax.ShapeDtypeStruct((size, wide), bf16)] * chunks
        + [
            jax.ShapeDtypeStruct((count, total), bf16),
            jax.ShapeDtypeStruct((topk, count), jnp.int32),
        ],
        compiler_params=pltpu.CompilerParams(vmem_limit_bytes=32 * MIB),
        name="dispatch",
    )(routing.T, replica.T, gates.T.astype(jnp.float32), host_expert.reshape(1, devices), tokens, grad_out)

    pieces = [spread(exchange(s)) for s in sent]
    half = size // 2

    def experts_of(c, experts):
        parts = pieces[c]
        rows = sum(p.shape[0] for p in parts)
        width = experts * quarter
        heights = [size] + [half] * 6
        gu_spec = [
            pl.BlockSpec((1, 2, quarter, features), lambda i, o, e=e: ((1 - 2 * e) * o[0] + e, 0, 0, 0))
            for e in range(experts)
        ]
        down_spec = [
            pl.BlockSpec((1, quarter, features), lambda i, o, e=e: ((1 - 2 * e) * o[0] + e, 0, 0))
            for e in range(experts)
        ]
        full = lambda h, w: pl.BlockSpec((h, w), lambda i, o: (0, 0))
        return pl.pallas_call(
            functools.partial(expert_kernel, experts, len(parts), len(heights)),
            grid_spec=pltpu.PrefetchScalarGridSpec(
                num_scalar_prefetch=1,
                grid=(1,),
                in_specs=[full(*p.shape) for p in parts] + gu_spec + down_spec,
                out_specs=[full(h, features + LANES) for h in heights]
                + [full(rows, 2 * width), full(rows, width)],
            ),
            out_shape=[jax.ShapeDtypeStruct((h, features + LANES), bf16) for h in heights]
            + [
                jax.ShapeDtypeStruct((rows, 2 * width), bf16),
                jax.ShapeDtypeStruct((rows, width), bf16),
            ],
            compiler_params=pltpu.CompilerParams(vmem_limit_bytes=48 * MIB),
            name=f"experts_{experts}",
        )(order, *parts, *[w_gate_up] * experts, *[w_down] * experts)

    *dx0, gm0, hg0 = experts_of(0, 1)
    *dx1, gm1, hg1 = experts_of(1, 2)

    steps = 4
    cut = features // steps
    n = len(pieces[0])
    x_spec = [pl.BlockSpec((p.shape[0], cut), lambda i, o: (0, i)) for p in pieces[0]]
    dy_spec = [pl.BlockSpec((p.shape[0], cut), lambda i, o: (0, i + steps)) for p in pieces[0]]
    full = lambda a: pl.BlockSpec(a.shape, lambda i, o: (0, 0))
    grad_gu, grad_down = pl.pallas_call(
        functools.partial(weights_kernel, n),
        grid_spec=pltpu.PrefetchScalarGridSpec(
            num_scalar_prefetch=1,
            grid=(steps,),
            in_specs=x_spec * 2 + dy_spec * 2 + [full(a) for a in (gm0, hg0, gm1, hg1)],
            out_specs=[
                pl.BlockSpec((owned, 2, quarter, cut), lambda i, o: (0, 0, 0, i)),
                pl.BlockSpec((owned, quarter, cut), lambda i, o: (0, 0, i)),
            ],
        ),
        out_shape=[
            jax.ShapeDtypeStruct(w_gate_up.shape, bf16),
            jax.ShapeDtypeStruct(w_down.shape, bf16),
        ],
        compiler_params=pltpu.CompilerParams(vmem_limit_bytes=40 * MIB),
        name="weights",
    )(order, *pieces[0], *pieces[1], *pieces[0], *pieces[1], gm0, hg0, gm1, hg1)

    home = [exchange(collect(*dx)) for dx in (dx0, dx1)]
    grad_tokens, grad_gates = pl.pallas_call(
        functools.partial(home_kernel, chunks),
        out_shape=[
            jax.ShapeDtypeStruct((count, features), bf16),
            jax.ShapeDtypeStruct((topk, count), jnp.float32),
        ],
        compiler_params=pltpu.CompilerParams(vmem_limit_bytes=16 * MIB),
        name="home",
    )(picker, slots, *home)
    return grad_tokens, grad_gates.T, grad_gu, grad_down


def solution(mesh):
    in_specs = (
        P(("dp", "expert"), None),
        P(("dp", "expert"), None),
        P(("dp", "expert"), None),
        P(("dp", "expert"), None),
        P(("dp", "expert"), None),
        P(),
        P("expert", None, "dp", None),
        P("expert", "dp", None),
    )
    out_specs = (
        P(("dp", "expert"), None),
        P(("dp", "expert"), None),
        P("expert", None, "dp", None),
        P("expert", "dp", None),
    )
    return jax.shard_map(shards, mesh=mesh, in_specs=in_specs, out_specs=out_specs, check_vma=False)
```

```python
import functools

import jax
import jax.numpy as jnp
from jax import lax
from jax.experimental import pallas as pl
from jax.experimental.pallas import tpu as pltpu
from jax.sharding import PartitionSpec as P

LANES = 128
MIB = 1 << 20
VMEM = 63 * MIB
EXPERTS_VMEM = 48 * MIB
NT = (((1,), (1,)), ((), ()))
TN = (((0,), (0,)), ((), ()))
NN = (((1,), (0,)), ((), ()))


def dot(a, b, dims):
    return lax.dot_general(a, b, dims, preferred_element_type=jnp.float32)


def iota(shape, dim):
    return lax.broadcasted_iota(jnp.int32, shape, dim)


def to_column(row):
    n = row.shape[1]
    eye = iota((n, n), 0) == iota((n, n), 1)
    return jnp.sum(jnp.where(eye, jnp.broadcast_to(row, (n, n)), 0), axis=1, keepdims=True)


def dispatch_kernel(
    chunks, devices, *refs
):
    inputs, outs, held, sems = refs[:6], refs[6:-7], refs[-7:-1], refs[-1]
    *row_refs, picker_ref, slots_ref = outs
    copies = [pltpu.make_async_copy(a, b, sems.at[i]) for i, (a, b) in enumerate(zip(inputs, held))]
    for copy in copies:
        copy.start()
    for copy in copies:
        copy.wait()
    routing, replica, gates, host, tokens, grad_out = held
    topk, count = routing.shape
    features = tokens.shape[1]
    total = topk * count
    per_pair = total // devices
    part = per_pair // chunks
    host_col = to_column(host[...])
    weights = gates[...].astype(jnp.float32)
    lanes_of = iota((count, total), 1)
    rows_of = iota((total, count), 0)
    gate_at = jnp.zeros((total, count), jnp.float32)
    first_at = jnp.zeros((total, count), jnp.float32)
    picked = jnp.zeros((total, count), jnp.float32)
    picked_t = jnp.zeros((count, total), jnp.float32)
    for k in range(topk):
        expert = routing[k : k + 1, :]
        dest = lax.shift_right_logical(expert, 1)
        listed = jnp.max((host_col == expert).astype(jnp.int32), axis=0, keepdims=True)
        usable = (replica[k : k + 1, :] == 0) | (listed > 0)
        key = (1 - listed) * count + iota((1, count), 1)
        dest_col, key_col = to_column(dest), to_column(key)
        ahead = (dest_col == dest) & (key_col < key)
        rank = jnp.sum(ahead.astype(jnp.int32), axis=0, keepdims=True)
        slot = (chunks - 1 - rank // part) * (devices * part) + dest * part + rank % part
        slot = jnp.where(usable, slot, -1)
        slots_ref[k : k + 1, :] = slot
        match = rows_of == slot
        picked = jnp.where(match, 1.0, picked)
        gate_at = jnp.where(match, weights[k : k + 1, :], gate_at)
        first_at = jnp.where(match, listed.astype(jnp.float32), first_at)
        picked_t = jnp.where(lanes_of == to_column(slot), 1.0, picked_t)
    picker_ref[...] = picked_t.astype(jnp.bfloat16)
    any_row = jnp.sum(picked, axis=1, keepdims=True)
    gate = jnp.sum(gate_at, axis=1, keepdims=True)
    first = jnp.sum(first_at, axis=1, keepdims=True)
    second = any_row - first
    lane = iota((total, LANES), 1)
    meta = jnp.where(lane == 0, gate * first, 0.0)
    meta = jnp.where(lane == 1, gate * second, meta)
    meta = jnp.where(lane == 2, first, meta)
    meta = jnp.where(lane == 3, second, meta).astype(jnp.bfloat16)
    picker = picked.astype(jnp.bfloat16)
    size = total // chunks
    for c, out in enumerate(row_refs):
        mine = slice(c * size, (c + 1) * size)
        out[:, :features] = dot(picker[mine], tokens[...], NN).astype(jnp.bfloat16)
        out[:, features : 2 * features] = dot(picker[mine], grad_out[...], NN).astype(jnp.bfloat16)
        out[:, 2 * features :] = meta[mine]


def pieces_of(refs, start, size, cols):
    got, at = [], 0
    for r in refs:
        low, high = max(start, at), min(start + size, at + r.shape[0])
        if low < high:
            got.append(r[low - at : high - at, cols])
        at += r.shape[0]
    return got[0] if len(got) == 1 else jnp.concatenate(got, axis=0)


def put_pieces(refs, start, cols, value):
    at = 0
    for r in refs:
        low, high = max(start, at), min(start + value.shape[0], at + r.shape[0])
        if low < high:
            r[low - at : high - at, cols] = value[low - start : high - start]
        at += r.shape[0]


def expert_kernel(experts, n_in, n_out, order, *refs):
    pieces = refs[:n_in]
    gu = refs[n_in : n_in + experts]
    down = refs[n_in + experts : n_in + 2 * experts]
    outs = refs[n_in + 2 * experts : n_in + 2 * experts + n_out]
    gm_ref, hg_ref = refs[n_in + 2 * experts + n_out :]
    quarter, features = down[0].shape[1:]
    width = experts * quarter
    rows = sum(p.shape[0] for p in pieces)

    def stack(parts):
        return parts[0] if experts == 1 else jnp.concatenate(parts, axis=0)

    w_gate = stack([w[0, 0] for w in gu])
    w_up = stack([w[0, 1] for w in gu])
    w_down = stack([w[0] for w in down])
    for at in range(0, rows, 256):
        block = min(256, rows - at)
        x = pieces_of(pieces, at, block, slice(0, features))
        dy = pieces_of(pieces, at, block, slice(features, 2 * features))
        meta = pieces_of(pieces, at, block, slice(2 * features, 2 * features + LANES)).astype(jnp.float32)
        weight, live = meta[:, 0:1], meta[:, 2:3]
        if experts == 2:
            is_first = iota((block, width), 1) < quarter
            weight = jnp.where(is_first, weight, meta[:, 1:2])
            live = jnp.where(is_first, live, meta[:, 3:4])
        gate = dot(x, w_gate, NT)
        up = dot(x, w_up, NT)
        back = dot(dy, w_down, NT)
        s = jax.nn.sigmoid(gate)
        active = gate * s
        hidden = (active * up).astype(jnp.bfloat16).astype(jnp.float32)
        dg = jnp.sum(hidden * back * live, axis=1, keepdims=True)
        grad_hidden = back * weight
        gm_gate = (grad_hidden * up * s * (1.0 + gate * (1.0 - s))).astype(jnp.bfloat16)
        gm_up = (grad_hidden * active).astype(jnp.bfloat16)
        gm_ref[at : at + block, :width] = gm_gate
        gm_ref[at : at + block, width:] = gm_up
        hg_ref[at : at + block] = (hidden * weight).astype(jnp.bfloat16)
        dx = dot(gm_gate, w_gate, NN) + dot(gm_up, w_up, NN)
        put_pieces(outs, at, slice(0, features), dx.astype(jnp.bfloat16))
        put_pieces(
            outs,
            at,
            slice(features, features + LANES),
            jnp.broadcast_to(dg, (block, LANES)).astype(jnp.bfloat16),
        )


def weights_kernel(n, n_grads, order, *refs):
    pieces, grads = refs[: 2 * n], refs[2 * n : 2 * n + n_grads]
    out_gu, out_down, held, sems = refs[2 * n + n_grads :]
    features = out_down.shape[2]
    size = pieces[0].shape[0]
    copies = []
    for side in range(2):
        cols = pl.ds(side * features, features)
        for i, p in enumerate(pieces):
            copies.append(
                pltpu.make_async_copy(p.at[:, cols], held.at[side, pl.ds(i * size, size)], sems.at[len(copies)])
            )
    for copy in copies:
        copy.start()
    both_gm, both_hg, one_gm, one_hg = grads[0:1], grads[1:2], grads[2::2], grads[3::2]
    q = one_hg[0].shape[1]
    middle = n * size
    first = order[0]
    second = 1 - first
    cut = 512

    def product(left, right):
        left = jnp.concatenate([p[...] for p in left], axis=0)
        return dot(left, right, TN)

    for copy in copies[: 2 * n]:
        copy.wait()
    for at in range(0, features, cut):
        cols = slice(at, at + cut)
        a, b = product(one_gm, held[0, middle:, cols]), product(both_gm, held[0, :middle, cols])
        for j in range(2):
            out_gu[first, j, :, cols] = (a[j * q : (j + 1) * q] + b[2 * j * q : (2 * j + 1) * q]).astype(jnp.bfloat16)
            out_gu[second, j, :, cols] = b[(2 * j + 1) * q : (2 * j + 2) * q].astype(jnp.bfloat16)
    for copy in copies[2 * n :]:
        copy.wait()
    for at in range(0, features, cut):
        cols = slice(at, at + cut)
        a, b = product(one_hg, held[1, middle:, cols]), product(both_hg, held[1, :middle, cols])
        out_down[first, :, cols] = (a + b[:q]).astype(jnp.bfloat16)
        out_down[second, :, cols] = b[q:].astype(jnp.bfloat16)


def home_kernel(chunks, picker, slots, *refs):
    rows, (tok_ref, gate_ref) = refs[:chunks], refs[chunks:]
    features = tok_ref.shape[1]
    topk, count = slots.shape
    size = rows[0].shape[0]
    total = jnp.zeros((count, features), jnp.float32)
    for c, r in enumerate(rows):
        total += dot(picker[:, c * size : (c + 1) * size], r[:, :features], NN)
    tok_ref[...] = total.astype(jnp.bfloat16)
    dg = jnp.concatenate([r[:, features : features + LANES] for r in rows], axis=0).astype(jnp.float32)[:, :1]
    rows_of = iota((chunks * size, count), 0)
    for k in range(topk):
        match = rows_of == slots[k : k + 1, :]
        gate_ref[k : k + 1, :] = jnp.sum(jnp.where(match, dg, 0.0), axis=0, keepdims=True)


def shift(x, step):
    n = lax.axis_size("dp")
    return lax.ppermute(x, "dp", [(i, (i + step) % n) for i in range(n)])


def after(value, *earlier):
    return lax.optimization_barrier((value, earlier))[0]


def add(a, b):
    return (a.astype(jnp.float32) + b.astype(jnp.float32)).astype(jnp.bfloat16)


def near(own):
    left_top, right_bottom = shift(own[0], 1), shift(own[1], -1)
    left_bottom, right_top = shift(own[1], 1), shift(own[0], -1)
    return (left_top, left_bottom), (right_top, right_bottom)


def add_up(*parts):
    return sum(p.astype(jnp.float32) for p in parts).astype(jnp.bfloat16)


def first_sums(left, right, far):
    far_top, far_bottom = shift(far[0], 1), shift(far[1], -1)
    return add(right[0], far_top), add(left[1], far_bottom)


def last_sums(own, left_top, right_bottom, to_right, to_left):
    from_right_top, from_left_bottom = shift(left_top, -1), shift(right_bottom, 1)
    from_left_top, from_right_bottom = shift(to_right, 1), shift(to_left, -1)
    return jnp.concatenate(
        [add_up(own[0], from_left_top, from_right_top), add_up(own[1], from_left_bottom, from_right_bottom)], axis=0
    )


def last_sums_whole(own, left_top, right_bottom, to_right, to_left):
    from_left = shift(jnp.concatenate([to_right, right_bottom], axis=0), 1)
    from_right = shift(jnp.concatenate([left_top, to_left], axis=0), -1)
    return add_up(jnp.concatenate(own, axis=0), from_left, from_right)


def by_device(x):
    devices = lax.axis_size("expert")
    return x.reshape(devices, x.shape[0] // devices, x.shape[1])


def exchange(x):
    return lax.all_to_all(x, "expert", split_axis=0, concat_axis=0, tiled=True)


def flat(x):
    return x.reshape(x.shape[0] * x.shape[1], x.shape[2])


def shards(tokens, grad_out, routing, replica, gates, host_expert, w_gate_up, w_down):
    devices = lax.axis_size("expert")
    device_id = lax.axis_index("expert")
    count, features = tokens.shape
    topk = routing.shape[1]
    owned, quarter = w_down.shape[:2]
    chunks = 2
    total = count * topk
    size = total // chunks
    wide = 2 * features + LANES
    bf16 = jnp.bfloat16

    first = jnp.sum(jnp.where(host_expert // owned == device_id, host_expert % owned, 0))
    order = first.astype(jnp.int32).reshape(1)

    *sent, picker, slots = pl.pallas_call(
        functools.partial(dispatch_kernel, chunks, devices),
        out_shape=[jax.ShapeDtypeStruct((size, wide), bf16)] * chunks
        + [
            jax.ShapeDtypeStruct((count, total), bf16),
            jax.ShapeDtypeStruct((topk, count), jnp.int32),
        ],
        in_specs=[pl.BlockSpec(memory_space=pltpu.HBM)] * 6,
        scratch_shapes=[pltpu.VMEM((topk, count), jnp.int32)] * 2
        + [
            pltpu.VMEM((topk, count), bf16),
            pltpu.VMEM((1, devices), jnp.int32),
            pltpu.VMEM((count, features), bf16),
            pltpu.VMEM((count, features), bf16),
            pltpu.SemaphoreType.DMA((6,)),
        ],
        compiler_params=pltpu.CompilerParams(vmem_limit_bytes=VMEM),
        name="dispatch",
    )(routing.T, replica.T, gates.T, host_expert.reshape(1, devices), tokens, grad_out)

    half = size // 2
    hbm = pl.BlockSpec(memory_space=pltpu.HBM)

    def experts_of(experts, *blocks):
        pieces = [p for block in blocks for p in block]
        n = len(pieces)
        width = experts * quarter
        rows = n * half
        shapes = [(half, features + LANES)] * n + [(rows, 2 * width), (rows, width)]
        gu_spec = [
            pl.BlockSpec((1, 2, quarter, features), lambda i, o, e=e: ((1 - 2 * e) * o[0] + e, 0, 0, 0))
            for e in range(experts)
        ]
        down_spec = [
            pl.BlockSpec((1, quarter, features), lambda i, o, e=e: ((1 - 2 * e) * o[0] + e, 0, 0))
            for e in range(experts)
        ]
        outs = pl.pallas_call(
            functools.partial(expert_kernel, experts, n, n),
            grid_spec=pltpu.PrefetchScalarGridSpec(
                num_scalar_prefetch=1,
                grid=(1,),
                in_specs=[pl.BlockSpec(p.shape, lambda i, o: (0, 0)) for p in pieces] + gu_spec + down_spec,
                out_specs=[pl.BlockSpec(s, lambda i, o: (0, 0)) for s in shapes],
            ),
            out_shape=[jax.ShapeDtypeStruct(s, bf16) for s in shapes],
            compiler_params=pltpu.CompilerParams(vmem_limit_bytes=EXPERTS_VMEM),
            name=f"experts_{experts}_{rows}",
        )(order, *pieces, *[w_gate_up] * experts, *[w_down] * experts)
        return [tuple(outs[2 * i : 2 * i + 2]) for i in range(n // 2)], outs[n:]

    def halves(raw):
        middle = devices // 2
        return flat(raw[:middle]), flat(raw[middle:])

    own0 = halves(exchange(by_device(sent[0])))
    left0, right0 = near(own0)
    far0_in = left0[0], right0[1]
    far0 = shift(far0_in[0], 1), shift(far0_in[1], -1)
    own1 = halves(after(exchange(by_device(sent[1])), far0_in))
    left1, right1 = near(own1)
    dx0, grads0 = experts_of(2, own0, left0, right0, far0)
    far1_in = after((left1[0], right1[1]), dx0[0])
    far1 = shift(far1_in[0], 1), shift(far1_in[1], -1)
    sums0 = first_sums(*dx0[1:])
    home0 = last_sums_whole(dx0[0], dx0[1][0], dx0[2][1], *sums0)
    dx1, grads1 = experts_of(1, own1, left1, right1)
    (dx1_far,), grads1_far = experts_of(1, after(far1, dx1[0]))
    dx1_far = after(dx1_far, sums0)
    sums1 = first_sums(*dx1[1:], dx1_far)
    home0 = by_device(home0)
    sums1 = after(sums1, home0)
    home1 = by_device(last_sums(dx1[0], dx1[1][0], dx1[2][1], *sums1))

    pieces = [p for block in (own0, left0, right0, far0, own1, left1, right1, far1) for p in block]
    n = len(pieces) // 2
    grads = [*grads0, *grads1, *grads1_far]
    grad_gu, grad_down = pl.pallas_call(
        functools.partial(weights_kernel, n, len(grads)),
        grid_spec=pltpu.PrefetchScalarGridSpec(
            num_scalar_prefetch=1,
            grid=(1,),
            in_specs=[hbm] * len(pieces) + [pl.BlockSpec(a.shape, lambda i, o: (0, 0)) for a in grads],
            out_specs=[
                pl.BlockSpec(w_gate_up.shape, lambda i, o: (0, 0, 0, 0)),
                pl.BlockSpec(w_down.shape, lambda i, o: (0, 0, 0)),
            ],
            scratch_shapes=[
                pltpu.VMEM((2, 2 * n * half, features), bf16),
                pltpu.SemaphoreType.DMA((4 * n,)),
            ],
        ),
        out_shape=[
            jax.ShapeDtypeStruct(w_gate_up.shape, bf16),
            jax.ShapeDtypeStruct(w_down.shape, bf16),
        ],
        compiler_params=pltpu.CompilerParams(vmem_limit_bytes=VMEM),
        name="weights",
    )(order, *pieces, *grads)

    home = [flat(exchange(home0)), flat(exchange(home1))]
    grad_tokens, grad_gates = pl.pallas_call(
        functools.partial(home_kernel, chunks),
        out_shape=[
            jax.ShapeDtypeStruct((count, features), bf16),
            jax.ShapeDtypeStruct((topk, count), jnp.float32),
        ],
        compiler_params=pltpu.CompilerParams(vmem_limit_bytes=16 * MIB),
        name="home",
    )(picker, slots, *home)
    return grad_tokens, grad_gates.T, grad_gu, grad_down


def solution(mesh):
    in_specs = (
        P(("dp", "expert"), None),
        P(("dp", "expert"), None),
        P(("dp", "expert"), None),
        P(("dp", "expert"), None),
        P(("dp", "expert"), None),
        P(),
        P("expert", None, "dp", None),
        P("expert", "dp", None),
    )
    out_specs = (
        P(("dp", "expert"), None),
        P(("dp", "expert"), None),
        P("expert", None, "dp", None),
        P("expert", "dp", None),
    )
    return jax.shard_map(shards, mesh=mesh, in_specs=in_specs, out_specs=out_specs, check_vma=False)
```

```python
import functools

import jax
import jax.numpy as jnp
from jax import lax
from jax.experimental import pallas as pl
from jax.experimental.pallas import tpu as pltpu
from jax.sharding import PartitionSpec as P

LANES = 128
MIB = 1 << 20
VMEM = 63 * MIB
EXPERTS_VMEM = 48 * MIB
NT = (((1,), (1,)), ((), ()))
TN = (((0,), (0,)), ((), ()))
NN = (((1,), (0,)), ((), ()))


def dot(a, b, dims):
    return lax.dot_general(a, b, dims, preferred_element_type=jnp.float32)


def iota(shape, dim):
    return lax.broadcasted_iota(jnp.int32, shape, dim)


def to_column(row):
    n = row.shape[1]
    eye = iota((n, n), 0) == iota((n, n), 1)
    return jnp.sum(jnp.where(eye, jnp.broadcast_to(row, (n, n)), 0), axis=1, keepdims=True)


def dispatch_kernel(
    chunks, devices, *refs
):
    inputs, outs, held, sems = refs[:6], refs[6:-7], refs[-7:-1], refs[-1]
    *row_refs, picker_ref, slots_ref = outs
    copies = [pltpu.make_async_copy(a, b, sems.at[i]) for i, (a, b) in enumerate(zip(inputs, held))]
    for copy in copies:
        copy.start()
    for copy in copies:
        copy.wait()
    routing, replica, gates, host, tokens, grad_out = held
    topk, count = routing.shape
    features = tokens.shape[1]
    total = topk * count
    per_pair = total // devices
    part = per_pair // chunks
    host_col = to_column(host[...])
    weights = gates[...].astype(jnp.float32)
    lanes_of = iota((count, total), 1)
    rows_of = iota((total, count), 0)
    gate_at = jnp.zeros((total, count), jnp.float32)
    first_at = jnp.zeros((total, count), jnp.float32)
    picked = jnp.zeros((total, count), jnp.float32)
    picked_t = jnp.zeros((count, total), jnp.float32)
    for k in range(topk):
        expert = routing[k : k + 1, :]
        dest = lax.shift_right_logical(expert, 1)
        listed = jnp.max((host_col == expert).astype(jnp.int32), axis=0, keepdims=True)
        usable = (replica[k : k + 1, :] == 0) | (listed > 0)
        key = (1 - listed) * count + iota((1, count), 1)
        dest_col, key_col = to_column(dest), to_column(key)
        ahead = (dest_col == dest) & (key_col < key)
        rank = jnp.sum(ahead.astype(jnp.int32), axis=0, keepdims=True)
        slot = (chunks - 1 - rank // part) * (devices * part) + dest * part + rank % part
        slot = jnp.where(usable, slot, -1)
        slots_ref[k : k + 1, :] = slot
        match = rows_of == slot
        picked = jnp.where(match, 1.0, picked)
        gate_at = jnp.where(match, weights[k : k + 1, :], gate_at)
        first_at = jnp.where(match, listed.astype(jnp.float32), first_at)
        picked_t = jnp.where(lanes_of == to_column(slot), 1.0, picked_t)
    picker_ref[...] = picked_t.astype(jnp.bfloat16)
    any_row = jnp.sum(picked, axis=1, keepdims=True)
    gate = jnp.sum(gate_at, axis=1, keepdims=True)
    first = jnp.sum(first_at, axis=1, keepdims=True)
    second = any_row - first
    lane = iota((total, LANES), 1)
    meta = jnp.where(lane == 0, gate * first, 0.0)
    meta = jnp.where(lane == 1, gate * second, meta)
    meta = jnp.where(lane == 2, first, meta)
    meta = jnp.where(lane == 3, second, meta).astype(jnp.bfloat16)
    picker = picked.astype(jnp.bfloat16)
    size = total // chunks
    for c, out in enumerate(row_refs):
        mine = slice(c * size, (c + 1) * size)
        out[:, :features] = dot(picker[mine], tokens[...], NN).astype(jnp.bfloat16)
        out[:, features : 2 * features] = dot(picker[mine], grad_out[...], NN).astype(jnp.bfloat16)
        out[:, 2 * features :] = meta[mine]


def pieces_of(refs, start, size, cols):
    got, at = [], 0
    for r in refs:
        low, high = max(start, at), min(start + size, at + r.shape[0])
        if low < high:
            got.append(r[low - at : high - at, cols])
        at += r.shape[0]
    return got[0] if len(got) == 1 else jnp.concatenate(got, axis=0)


def put_pieces(refs, start, cols, value):
    at = 0
    for r in refs:
        low, high = max(start, at), min(start + value.shape[0], at + r.shape[0])
        if low < high:
            r[low - at : high - at, cols] = value[low - start : high - start]
        at += r.shape[0]


def expert_kernel(experts, n_in, n_out, order, *refs):
    pieces = refs[:n_in]
    gu = refs[n_in : n_in + experts]
    down = refs[n_in + experts : n_in + 2 * experts]
    outs = refs[n_in + 2 * experts : n_in + 2 * experts + n_out]
    gm_ref, hg_ref = refs[n_in + 2 * experts + n_out :]
    quarter, features = down[0].shape[1:]
    width = experts * quarter
    rows = sum(p.shape[0] for p in pieces)

    def stack(parts):
        return parts[0] if experts == 1 else jnp.concatenate(parts, axis=0)

    w_gate = stack([w[0, 0] for w in gu])
    w_up = stack([w[0, 1] for w in gu])
    w_down = stack([w[0] for w in down])
    for at in range(0, rows, 256):
        block = min(256, rows - at)
        x = pieces_of(pieces, at, block, slice(0, features))
        dy = pieces_of(pieces, at, block, slice(features, 2 * features))
        meta = pieces_of(pieces, at, block, slice(2 * features, 2 * features + LANES)).astype(jnp.float32)
        weight, live = meta[:, 0:1], meta[:, 2:3]
        if experts == 2:
            is_first = iota((block, width), 1) < quarter
            weight = jnp.where(is_first, weight, meta[:, 1:2])
            live = jnp.where(is_first, live, meta[:, 3:4])
        gate = dot(x, w_gate, NT)
        up = dot(x, w_up, NT)
        back = dot(dy, w_down, NT)
        s = jax.nn.sigmoid(gate)
        active = gate * s
        hidden = (active * up).astype(jnp.bfloat16).astype(jnp.float32)
        dg = jnp.sum(hidden * back * live, axis=1, keepdims=True)
        grad_hidden = back * weight
        gm_gate = (grad_hidden * up * s * (1.0 + gate * (1.0 - s))).astype(jnp.bfloat16)
        gm_up = (grad_hidden * active).astype(jnp.bfloat16)
        gm_ref[at : at + block, :width] = gm_gate
        gm_ref[at : at + block, width:] = gm_up
        hg_ref[at : at + block] = (hidden * weight).astype(jnp.bfloat16)
        dx = dot(gm_gate, w_gate, NN) + dot(gm_up, w_up, NN)
        put_pieces(outs, at, slice(0, features), dx.astype(jnp.bfloat16))
        put_pieces(
            outs,
            at,
            slice(features, features + LANES),
            jnp.broadcast_to(dg, (block, LANES)).astype(jnp.bfloat16),
        )


def weights_kernel(n, n_grads, order, *refs):
    pieces, grads = refs[: 2 * n], refs[2 * n : 2 * n + n_grads]
    out_gu, out_down, held, sems = refs[2 * n + n_grads :]
    features = out_down.shape[2]
    size = pieces[0].shape[0]
    copies = []
    for side in range(2):
        cols = pl.ds(side * features, features)
        for i, p in enumerate(pieces):
            copies.append(
                pltpu.make_async_copy(p.at[:, cols], held.at[side, pl.ds(i * size, size)], sems.at[len(copies)])
            )
    for copy in copies:
        copy.start()
    both_gm, both_hg, one_gm, one_hg = grads[0:1], grads[1:2], grads[2::2], grads[3::2]
    q = one_hg[0].shape[1]
    middle = n * size
    first = order[0]
    second = 1 - first
    cut = 512

    def product(left, right):
        left = jnp.concatenate([p[...] for p in left], axis=0)
        return dot(left, right, TN)

    for copy in copies[: 2 * n]:
        copy.wait()
    for at in range(0, features, cut):
        cols = slice(at, at + cut)
        a, b = product(one_gm, held[0, middle:, cols]), product(both_gm, held[0, :middle, cols])
        for j in range(2):
            out_gu[first, j, :, cols] = (a[j * q : (j + 1) * q] + b[2 * j * q : (2 * j + 1) * q]).astype(jnp.bfloat16)
            out_gu[second, j, :, cols] = b[(2 * j + 1) * q : (2 * j + 2) * q].astype(jnp.bfloat16)
    for copy in copies[2 * n :]:
        copy.wait()
    for at in range(0, features, cut):
        cols = slice(at, at + cut)
        a, b = product(one_hg, held[1, middle:, cols]), product(both_hg, held[1, :middle, cols])
        out_down[first, :, cols] = (a + b[:q]).astype(jnp.bfloat16)
        out_down[second, :, cols] = b[q:].astype(jnp.bfloat16)


def home_kernel(chunks, picker, slots, *refs):
    rows, (tok_ref, gate_ref) = refs[:chunks], refs[chunks:]
    features = tok_ref.shape[1]
    topk, count = slots.shape
    size = rows[0].shape[0]
    total = jnp.zeros((count, features), jnp.float32)
    for c, r in enumerate(rows):
        total += dot(picker[:, c * size : (c + 1) * size], r[:, :features], NN)
    tok_ref[...] = total.astype(jnp.bfloat16)
    dg = jnp.concatenate([r[:, features : features + LANES] for r in rows], axis=0).astype(jnp.float32)[:, :1]
    rows_of = iota((chunks * size, count), 0)
    for k in range(topk):
        match = rows_of == slots[k : k + 1, :]
        gate_ref[k : k + 1, :] = jnp.sum(jnp.where(match, dg, 0.0), axis=0, keepdims=True)


def shift(x, step):
    n = lax.axis_size("dp")
    return lax.ppermute(x, "dp", [(i, (i + step) % n) for i in range(n)])


def after(value, *earlier):
    return lax.optimization_barrier((value, earlier))[0]


def add(a, b):
    return (a.astype(jnp.float32) + b.astype(jnp.float32)).astype(jnp.bfloat16)


def near(own):
    left_top, right_bottom = shift(own[0], 1), shift(own[1], -1)
    left_bottom, right_top = shift(own[1], 1), shift(own[0], -1)
    return (left_top, left_bottom), (right_top, right_bottom)


def add_up(*parts):
    return sum(p.astype(jnp.float32) for p in parts).astype(jnp.bfloat16)


def first_sums(left, right, far):
    far_top, far_bottom = shift(far[0], 1), shift(far[1], -1)
    return add(right[0], far_top), add(left[1], far_bottom)


def last_sums(own, left_top, right_bottom, to_right, to_left):
    from_right_top, from_left_bottom = shift(left_top, -1), shift(right_bottom, 1)
    from_left_top, from_right_bottom = shift(to_right, 1), shift(to_left, -1)
    return jnp.concatenate(
        [add_up(own[0], from_left_top, from_right_top), add_up(own[1], from_left_bottom, from_right_bottom)], axis=0
    )


def last_sums_whole(own, left_top, right_bottom, to_right, to_left):
    from_left = shift(jnp.concatenate([to_right, right_bottom], axis=0), 1)
    from_right = shift(jnp.concatenate([left_top, to_left], axis=0), -1)
    return add_up(jnp.concatenate(own, axis=0), from_left, from_right)


def by_device(x):
    devices = lax.axis_size("expert")
    return x.reshape(devices, x.shape[0] // devices, x.shape[1])


def exchange(x):
    return lax.all_to_all(x, "expert", split_axis=0, concat_axis=0, tiled=True)


def flat(x):
    return x.reshape(x.shape[0] * x.shape[1], x.shape[2])


def shards(tokens, grad_out, routing, replica, gates, host_expert, w_gate_up, w_down):
    devices = lax.axis_size("expert")
    device_id = lax.axis_index("expert")
    count, features = tokens.shape
    topk = routing.shape[1]
    owned, quarter = w_down.shape[:2]
    chunks = 2
    total = count * topk
    size = total // chunks
    wide = 2 * features + LANES
    bf16 = jnp.bfloat16

    first = jnp.sum(jnp.where(host_expert // owned == device_id, host_expert % owned, 0))
    order = first.astype(jnp.int32).reshape(1)

    *sent, picker, slots = pl.pallas_call(
        functools.partial(dispatch_kernel, chunks, devices),
        out_shape=[jax.ShapeDtypeStruct((size, wide), bf16)] * chunks
        + [
            jax.ShapeDtypeStruct((count, total), bf16),
            jax.ShapeDtypeStruct((topk, count), jnp.int32),
        ],
        in_specs=[pl.BlockSpec(memory_space=pltpu.HBM)] * 6,
        scratch_shapes=[pltpu.VMEM((topk, count), jnp.int32)] * 2
        + [
            pltpu.VMEM((topk, count), bf16),
            pltpu.VMEM((1, devices), jnp.int32),
            pltpu.VMEM((count, features), bf16),
            pltpu.VMEM((count, features), bf16),
            pltpu.SemaphoreType.DMA((6,)),
        ],
        compiler_params=pltpu.CompilerParams(vmem_limit_bytes=VMEM),
        name="dispatch",
    )(routing.T, replica.T, gates.T, host_expert.reshape(1, devices), tokens, grad_out)

    half = size // 2
    hbm = pl.BlockSpec(memory_space=pltpu.HBM)

    def experts_of(experts, *blocks):
        pieces = [p for block in blocks for p in block]
        n = len(pieces)
        width = experts * quarter
        rows = n * half
        shapes = [(half, features + LANES)] * n + [(rows, 2 * width), (rows, width)]
        gu_spec = [
            pl.BlockSpec((1, 2, quarter, features), lambda i, o, e=e: ((1 - 2 * e) * o[0] + e, 0, 0, 0))
            for e in range(experts)
        ]
        down_spec = [
            pl.BlockSpec((1, quarter, features), lambda i, o, e=e: ((1 - 2 * e) * o[0] + e, 0, 0))
            for e in range(experts)
        ]
        outs = pl.pallas_call(
            functools.partial(expert_kernel, experts, n, n),
            grid_spec=pltpu.PrefetchScalarGridSpec(
                num_scalar_prefetch=1,
                grid=(1,),
                in_specs=[pl.BlockSpec(p.shape, lambda i, o: (0, 0)) for p in pieces] + gu_spec + down_spec,
                out_specs=[pl.BlockSpec(s, lambda i, o: (0, 0)) for s in shapes],
            ),
            out_shape=[jax.ShapeDtypeStruct(s, bf16) for s in shapes],
            compiler_params=pltpu.CompilerParams(vmem_limit_bytes=EXPERTS_VMEM),
            name=f"experts_{experts}_{rows}",
        )(order, *pieces, *[w_gate_up] * experts, *[w_down] * experts)
        return [tuple(outs[2 * i : 2 * i + 2]) for i in range(n // 2)], outs[n:]

    def halves(raw):
        middle = devices // 2
        return flat(raw[:middle]), flat(raw[middle:])

    own0 = halves(exchange(by_device(sent[0])))
    left0, right0 = near(own0)
    far0_in = left0[0], right0[1]
    far0 = shift(far0_in[0], 1), shift(far0_in[1], -1)
    own1 = halves(after(exchange(by_device(sent[1])), far0_in))
    left1, right1 = near(own1)
    dx0, grads0 = experts_of(2, own0, left0, right0, far0)
    far1_in = after((left1[0], right1[1]), dx0[0])
    far1 = shift(far1_in[0], 1), shift(far1_in[1], -1)
    sums0 = first_sums(*dx0[1:])
    home0 = last_sums_whole(dx0[0], dx0[1][0], dx0[2][1], *sums0)
    dx1, grads1 = experts_of(1, own1, left1, right1)
    (dx1_far,), grads1_far = experts_of(1, after(far1, dx1[0]))
    dx1_far = after(dx1_far, sums0)
    sums1 = first_sums(*dx1[1:], dx1_far)
    home1 = last_sums(dx1[0], dx1[1][0], dx1[2][1], *sums1)

    pieces = [p for block in (own0, left0, right0, far0, own1, left1, right1, far1) for p in block]
    n = len(pieces) // 2
    grads = [*grads0, *grads1, *grads1_far]
    grad_gu, grad_down = pl.pallas_call(
        functools.partial(weights_kernel, n, len(grads)),
        grid_spec=pltpu.PrefetchScalarGridSpec(
            num_scalar_prefetch=1,
            grid=(1,),
            in_specs=[hbm] * len(pieces) + [pl.BlockSpec(a.shape, lambda i, o: (0, 0)) for a in grads],
            out_specs=[
                pl.BlockSpec(w_gate_up.shape, lambda i, o: (0, 0, 0, 0)),
                pl.BlockSpec(w_down.shape, lambda i, o: (0, 0, 0)),
            ],
            scratch_shapes=[
                pltpu.VMEM((2, 2 * n * half, features), bf16),
                pltpu.SemaphoreType.DMA((4 * n,)),
            ],
        ),
        out_shape=[
            jax.ShapeDtypeStruct(w_gate_up.shape, bf16),
            jax.ShapeDtypeStruct(w_down.shape, bf16),
        ],
        compiler_params=pltpu.CompilerParams(vmem_limit_bytes=VMEM),
        name="weights",
    )(order, *pieces, *grads)

    both = jnp.concatenate([by_device(home0), by_device(home1)], axis=1)
    both = exchange(both)
    home = [flat(both[:, : size // devices]), flat(both[:, size // devices :])]
    grad_tokens, grad_gates = pl.pallas_call(
        functools.partial(home_kernel, chunks),
        out_shape=[
            jax.ShapeDtypeStruct((count, features), bf16),
            jax.ShapeDtypeStruct((topk, count), jnp.float32),
        ],
        compiler_params=pltpu.CompilerParams(vmem_limit_bytes=16 * MIB),
        name="home",
    )(picker, slots, *home)
    return grad_tokens, grad_gates.T, grad_gu, grad_down


def solution(mesh):
    in_specs = (
        P(("dp", "expert"), None),
        P(("dp", "expert"), None),
        P(("dp", "expert"), None),
        P(("dp", "expert"), None),
        P(("dp", "expert"), None),
        P(),
        P("expert", None, "dp", None),
        P("expert", "dp", None),
    )
    out_specs = (
        P(("dp", "expert"), None),
        P(("dp", "expert"), None),
        P("expert", None, "dp", None),
        P("expert", "dp", None),
    )
    return jax.shard_map(shards, mesh=mesh, in_specs=in_specs, out_specs=out_specs, check_vma=False)
```
